32 devices in a mesh: grp: 1, col: 32 (over z, y, x, core), row: 1.
Axes of the slice: x: 2, y: 2, z: 4, core: 2. Of those that a mesh axis runs over, the one named last changes fastest.
Arguments:
- activations: bfloat16 [4096, 7168], P(('grp', 'col'), 'row'), may hold values from -6 to 6
- out_grads: bfloat16 [4096, 4096], P(('grp', 'col')), may hold values from -6 to 6
- in_basis: bfloat16 [7168, 7168], P('row', 'col'), may hold values from -0.0625 to 0.0625
- out_basis: bfloat16 [4096, 4096], P('col', 'row'), may hold values from -0.09375 to 0.09375
- eigen_values: float32 [4096, 7168], P('row', 'col'), may hold values from 0.1 to 10
- queries: bfloat16 [2, 4096, 7168], P(None, 'row', 'col'), may hold values from -0.00390625 to 0.00390625
- doc_ids: int32 [4096], P('grp'), may hold values from 0 to 63, never falling along the last dimension, each value on 1 to 128 neighbouring positions
Outputs:
- scores: float32 [64, 2], P('grp')
The draws below stay inside these ranges and needn't reach their ends.
Inputs may be any that keep to these rules, and one draw needn't show every extreme that they name: doc_ids is non-decreasing along the tokens; each of the 64 documents has 1 to 128 tokens, and one has exactly 128.
All inputs are finite; a program needn't handle non-finite values.
Results may differ from the reference program's by a relative error of at most 0.0057.
Values may be sent and summed in bfloat16 or wider, within the bound.
No kernel may reach another device: no remote copies, remote signals or barrier semaphores. Data moves between devices by JAX's collectives and lax.ppermute only.
A program may use at most 192 MiB of HBM per device.

```python
import math
import jax
import jax.numpy as jnp
import numpy as np
from jax import lax

D = 4096
FF = 7168
NQ = 2
TOKENS = 4096
NDOC = 64
DOC_MOST = 128


def block_scale(rng, extent, shards, low, top_value):
    factor_of, own = 1.0, jax.random.fold_in(rng, 6)
    for dim, shards_of in shards:
        heights = jnp.exp(jax.random.uniform(jax.random.fold_in(own, dim), (shards_of,), jnp.float32, low / len(shards), top_value / len(shards)))
        factor_of = factor_of * jnp.repeat(heights, extent[dim] // shards_of).reshape([-1 if axis == dim else 1 for axis in range(len(extent))])
    return factor_of


def split_up(amount, total, bound, lean):
    portions = [(1 << 20) // math.isqrt(grade ** lean) + 1 for grade in range(2, amount + 1)]
    rest, given = total - bound - (amount - 1), [1] * (amount - 1)
    while rest > 0:
        candidates = [i for i in range(amount - 1) if given[i] < bound]
        pool, budget = sum([portions[i] for i in candidates]), rest
        for i in candidates:
            more = min(bound - given[i], max(1, budget * portions[i] // pool), rest)
            given[i] = given[i] + more
            rest = rest - more
    return np.array([bound] + given)


def uneven_parts(own_key, count, total, most, skew):
    if count == 2:
        one = jax.random.randint(own_key, (), max(1, total - most), min(most, total - 1) + 1)
        return jnp.stack([one, total - one])
    lengths = jnp.asarray(split_up(count, total, most, skew), jnp.int32)
    pairs = (count - 1) // 2
    source_of, sink = lengths[1:1 + 2 * pairs:2], lengths[2:2 + 2 * pairs:2]
    room = jnp.minimum(source_of - 1, most - sink)
    passed = jax.random.randint(jax.random.fold_in(own_key, 1), (pairs,), 0, 1 << 20) % (room + 1)
    lengths = lengths.at[1:1 + 2 * pairs:2].set(source_of - passed).at[2:2 + 2 * pairs:2].set(sink + passed)
    return lengths[jax.random.permutation(jax.random.fold_in(own_key, 2), count)]


def centred(rng, dims, scale, most, pieces=(), held_as=jnp.bfloat16):
    entries = scale * jax.random.normal(rng, dims, jnp.float32)
    if pieces:
        entries = entries * block_scale(rng, dims, pieces, -0.22, 0.18)
    return jnp.clip(entries, -most, most).astype(held_as)


def setup_inputs(seed: int = 0, part: int = 0) -> dict:
    key_list = jax.random.split(jax.random.key(seed), 8)
    part_splits = jax.random.split(jax.random.fold_in(key_list[7], part), 8)
    activations = centred(part_splits[0], (TOKENS, FF), 1.0, 6.0, ((0, 32),))
    out_grads = centred(part_splits[1], (TOKENS, D), 1.0, 6.0, ((0, 32),))
    in_basis = centred(key_list[2], (FF, FF), FF ** -0.5, 0.0625, ((1, 32),))
    out_basis = centred(key_list[3], (D, D), D ** -0.5, 0.09375, ((0, 32),))
    eigen_values = jnp.clip(jnp.exp(math.log(10.0) - 4.6051702 * jax.random.uniform(key_list[4], (D, FF), jnp.float32) ** block_scale(key_list[4], (D, FF), ((1, 32),), -0.2, 0.2)), 0.1, 10.0)
    queries = centred(key_list[5], (NQ, D, FF), (D * FF // 16) ** -0.5, 0.00390625, ((2, 32),))
    doc_ids = jnp.searchsorted(jnp.cumsum(uneven_parts(part_splits[6], NDOC, TOKENS, DOC_MOST, 0)), jnp.arange(TOKENS), side="right").astype(jnp.int32)
    return dict(activations=activations, out_grads=out_grads, in_basis=in_basis, out_basis=out_basis, eigen_values=eigen_values, queries=queries, doc_ids=doc_ids)


damping = 0.1


def reference(activations, out_grads, in_basis, out_basis, eigen_values, queries, doc_ids):
    act_rot = jnp.dot(activations, in_basis, preferred_element_type=jnp.float32).astype(jnp.bfloat16)
    grad_rot = jnp.dot(out_grads, out_basis, preferred_element_type=jnp.float32).astype(jnp.bfloat16)
    inverse_scale = 1.0 / (eigen_values + damping)
    act_wide = act_rot.astype(jnp.float32)

    def per_query(query_grad):
        scaled = (query_grad.astype(jnp.float32) * inverse_scale).astype(jnp.bfloat16)
        projected = jnp.dot(grad_rot, scaled, preferred_element_type=jnp.float32)
        return jnp.sum(projected * act_wide, axis=1)

    token_scores = lax.map(per_query, queries).T
    membership = (doc_ids[:, None] == jnp.arange(NDOC, dtype=jnp.int32)[None, :]).astype(jnp.float32)
    doc_sizes = jnp.sum(membership, axis=0)
    summed = jnp.dot(membership.T, token_scores, precision=lax.Precision.HIGHEST, preferred_element_type=jnp.float32)
    return summed / doc_sizes[:, None]
```

```python
import jax
import jax.numpy as jnp
from jax import lax
from jax.sharding import PartitionSpec as P

damping = 0.1


def roles(n):
    bits = n.bit_length() - 1
    if bits >= 4:
        tokens = [0, bits - 2]
    else:
        tokens = [0] if bits else []
    columns = [b for b in range(bits) if b not in tokens]
    return tokens, columns


def swap(value, bit, n):
    return lax.ppermute(value, "col", [(d, d ^ (1 << bit)) for d in range(n)])


def dotf(a, b, dims):
    return lax.dot_general(a, b, (dims, ((), ())), preferred_element_type=jnp.float32)


def spread(value, columns, n):
    pieces = {0: value}
    top = len(columns) - 1
    order = sorted(range(1, 1 << len(columns)), key=lambda e: (bin(e).count("1"), e))
    for e in order:
        has = [i for i in range(top + 1) if e >> i & 1]
        if e >> top & 1:
            last = has[0]
        else:
            last = has[-1]
        pieces[e] = swap(pieces[e ^ (1 << last)], columns[last], n)
    return [pieces[e] for e in range(1 << len(columns))]


def make_local(n):
    tokens, columns = roles(n)
    groups = 1 << len(columns)

    def offset(e):
        return sum((1 << columns[i]) for i in range(len(columns)) if e >> i & 1)

    def local(activations, out_grads, in_basis, out_basis, eigen_values, queries, doc_ids):
        me = lax.axis_index("col")
        part = sum(((me >> b) & 1) << i for i, b in enumerate(columns))
        rows = out_basis.shape[0]
        wide = out_basis.shape[1] // groups
        mine = activations.shape[0]

        grads = spread(out_grads, columns, n)
        block = out_basis
        for b in reversed(columns):
            bit = ((me >> b) & 1) == 0
            half = block.shape[1] // 2
            low, high = block[:, :half], block[:, half:]
            keep = jnp.where(bit, low, high)
            came = swap(jnp.where(bit, high, low), b, n)
            block = jnp.concatenate([jnp.where(bit, keep, came), jnp.where(bit, came, keep)], axis=0)
        majors = list(reversed(columns))
        for b in reversed(tokens):
            bit = ((me >> b) & 1) == 0
            came = swap(block, b, n)
            block = jnp.concatenate([jnp.where(bit, block, came), jnp.where(bit, came, block)], axis=0)
            majors.append(b)
        majors = majors[::-1]
        block = block.reshape((2,) * len(majors) + (rows, wide))
        where = [majors.index(b) for b in sorted(majors, reverse=True)]
        block = block.transpose(where + [len(majors), len(majors) + 1]).reshape(n * rows, wide)
        rotated = dotf(jnp.concatenate(grads, axis=0), block, ((1,), (0,))).astype(jnp.bfloat16)
        pieces = spread(rotated, columns, n)
        pieces = [
            jnp.concatenate([p[(r ^ e) * mine : (r ^ e) * mine + mine] for r in range(groups)], axis=0)
            for e, p in enumerate(pieces)
        ]
        grad_rot = jnp.concatenate(pieces, axis=1)

        values, grads_q = eigen_values.T, queries.transpose(0, 2, 1)
        scaled = []
        for e in range(groups):
            start = (part ^ e) * wide
            inverse = 1.0 / (lax.dynamic_slice_in_dim(values, start, wide, 1) + damping)
            piece = lax.dynamic_slice_in_dim(grads_q, start, wide, 2).astype(jnp.float32)
            scaled.append((piece * inverse[None]).astype(jnp.bfloat16))
        scaled = jnp.concatenate(scaled, axis=2)

        bases, weights = [in_basis.T], [scaled]
        for b in reversed(tokens):
            bases = bases + [swap(v, b, n) for v in bases]
            weights = weights + [swap(v, b, n) for v in weights]
        basis = jnp.concatenate(bases, axis=0)
        queries_n, span = queries.shape[0], basis.shape[0]
        weight = jnp.concatenate([w[q] for q in range(queries_n) for w in weights], axis=0)

        acts = spread(activations, columns, n)
        full, top = groups - 1, groups >> 1
        order = sorted(range(groups), key=lambda e: (bin(e).count("1"), e))
        pairs = [order[i : i + 2] for i in range(0, groups, 2)]
        token_part, ids = [], []
        for pair in pairs:
            act = jnp.concatenate([acts[e] for e in pair], axis=0)
            act_rot = lax.psum(dotf(act, basis, ((1,), (1,))), "row")
            act_rot = act_rot.astype(jnp.bfloat16).astype(jnp.float32)
            rot = jnp.concatenate([grad_rot[e * mine : e * mine + mine] for e in pair], axis=0)
            mixed = dotf(rot, weight, ((1,), (1,)))
            token_part.append(
                jnp.stack(
                    [jnp.sum(mixed[:, q * span : (q + 1) * span] * act_rot, axis=1) for q in range(queries_n)], axis=1
                )
            )
            ids += [lax.dynamic_slice_in_dim(doc_ids, (me ^ offset(e)) * mine, mine) for e in pair]
        token_part = jnp.concatenate(token_part, axis=0)
        ids = jnp.concatenate(ids)

        docs = jnp.arange(max(2, doc_ids.shape[0] // 64), dtype=jnp.int32)
        doc_sizes = jnp.sum((doc_ids[:, None] == docs[None, :]).astype(jnp.float32), axis=0)
        membership = (ids[:, None] == docs[None, :]).astype(jnp.float32)
        summed = jnp.dot(
            membership.T, token_part, precision=lax.Precision.HIGHEST, preferred_element_type=jnp.float32
        )
        for b in range(len(tokens) + len(columns)):
            summed = summed + swap(summed, b, n)
        return lax.psum(summed, "row") / doc_sizes[:, None]

    return local


def solution(mesh):
    placed = (
        P(("grp", "col"), "row"),
        P(("grp", "col"), None),
        P("row", "col"),
        P("col", "row"),
        P("row", "col"),
        P(None, "row", "col"),
        P("grp"),
    )
    return jax.shard_map(
        make_local(mesh.shape["col"]), mesh=mesh, in_specs=placed, out_specs=P("grp", None), check_vma=False
    )
```
